32 devices in a mesh: dp: 8 (over z, x), ctx: 4 (over y, core).
Axes of the slice: x: 2, y: 2, z: 4, core: 2. Of those that a mesh axis runs over, the one named last changes fastest.
Arguments:
- query: bfloat16 [16, 256, 4096], P('dp', 'ctx'), may hold values from -6 to 6
- key_in: bfloat16 [16, 256, 1024], P('dp', 'ctx'), may hold values from -6 to 6
- value_in: bfloat16 [16, 256, 1024], P('dp', 'ctx'), may hold values from -6 to 6
- out_grad: bfloat16 [16, 256, 4096], P('dp', 'ctx'), may hold values from -1.5 to 1.5
- masked: int32 [16, 128], P('dp'), may hold values from 0 to 255, as said below
- bucket: int32 [16, 256], P('dp', 'ctx'), may hold values from 0 to 15
Outputs:
- query_grad: bfloat16 [16, 256, 4096], P('dp', 'ctx')
- key_grad: bfloat16 [16, 256, 1024], P('dp', 'ctx')
- value_grad: bfloat16 [16, 256, 1024], P('dp', 'ctx')
- bias_query_grad: float32 [4, 1024], P('ctx', 'dp')
- bias_kv_grad: float32 [2, 1024], P(None, 'dp')
The draws below stay inside these ranges and needn't reach their ends.
Inputs may be any that keep to these rules, and one draw needn't show every extreme that they name: Each document has exactly 128 distinct masked positions.
All inputs are finite; a program needn't handle non-finite values.
Results may differ from the reference program's by a relative error of at most 0.012.
The reference program's roundings to bfloat16 on the way count: a program that leaves them out, or rounds other values in their place, can miss the bound.
Values may be sent and summed in bfloat16 or wider, within the bound.
No kernel may reach another device: no remote copies, remote signals or barrier semaphores. Data moves between devices by JAX's collectives and lax.ppermute only.
A program may use at most 64 MiB of HBM per device.

```python
import math
import jax
import jax.numpy as jnp
from jax import lax

H = 32
KVH = 8
HD = 128
NB = 16
L = 256
DOCS = 16
MASKED = 128
N_CTX = 4


def draw_query(key, part):
    normal_part = jnp.clip(jax.random.normal(jax.random.fold_in(key, 1), (DOCS, L, H * HD), jnp.float32), -6.0, 6.0)
    return normal_part.astype(jnp.bfloat16)


def draw_key_in(key, part):
    normal_part = jnp.clip(jax.random.normal(jax.random.fold_in(key, 3), (DOCS, L, KVH * HD), jnp.float32), -6.0, 6.0)
    return normal_part.astype(jnp.bfloat16)


def draw_masked(key, part):
    doc_keys = jax.random.split(jax.random.fold_in(key, 7), DOCS)
    orders = jax.vmap(lambda one_key: jax.random.permutation(one_key, L))(doc_keys)
    return orders[:, :MASKED].astype(jnp.int32)


def with_ends(result, own_key, least, top_value):
    shape = result.shape
    place = [jax.random.randint(jax.random.fold_in(own_key, axis), (), 0, shape[axis]) for axis in range(len(shape))]
    result = result.at[tuple(place)].set(least)
    longest = shape.index(max(shape))
    place[longest] = (place[longest] + 1) % shape[longest]
    return result.at[tuple(place)].set(top_value)


def shard_levels(own_key, shape, pieces, least, high):
    loudness = 1.0
    for position, parts in pieces:
        draws = jax.random.uniform(jax.random.fold_in(jax.random.fold_in(own_key, 6), position), (parts,), jnp.float32, least / len(pieces), high / len(pieces))
        loudness = loudness * jnp.repeat(jnp.exp(draws), shape[position] // parts).reshape((-1,) + (1,) * (len(shape) - 1 - position))
    return loudness


def centred(own_key, dims, scale, reach, cuts=(), held_as=jnp.bfloat16):
    drawn = scale * jax.random.normal(own_key, dims, jnp.float32)
    if cuts:
        drawn = drawn * shard_levels(own_key, dims, cuts, -0.22, 0.18)
    return jnp.clip(drawn, -reach, reach).astype(held_as)


def setup_inputs(seed: int = 0) -> dict:
    splits = jax.random.split(jax.random.key(seed), 7)
    return {
        "query": draw_query(jax.random.fold_in(splits[6], 71), 0),
        "key_in": draw_key_in(jax.random.fold_in(splits[6], 71), 0),
        "value_in": centred(splits[2], (DOCS, L, KVH * HD), 1.0, 6.0, ((0, 8), (1, 4))),
        "out_grad": centred(splits[3], (DOCS, L, H * HD), 0.25, 1.5, ((0, 8), (1, 4))),
        "masked": draw_masked(jax.random.fold_in(splits[6], 71), 0),
        "bucket": with_ends(jax.random.randint(splits[5], (DOCS, L), 0, NB), jax.random.fold_in(splits[5], 1), 0, NB - 1).astype(jnp.int32),
    }


def softmax_rows(scores):
    shifted = scores - lax.optimization_barrier(jnp.max(scores, axis=-1, keepdims=True))
    exponent = jnp.exp(shifted)
    return exponent / lax.optimization_barrier(jnp.sum(exponent, axis=-1, keepdims=True))

def head_group(inputs):
    queries, key_one, value_one, cot_group = inputs
    inv_root = 1.0 / math.sqrt(HD)
    query_float = queries.astype(jnp.float32)
    key_float = key_one.astype(jnp.float32)
    value_float = value_one.astype(jnp.float32)
    cot_float = cot_group.astype(jnp.float32)
    scores = jnp.einsum('hqd,kd->hqk', query_float, key_float) * inv_root
    attn_probs = softmax_rows(scores)
    probs_float = lax.optimization_barrier(attn_probs.astype(jnp.bfloat16)).astype(jnp.float32)
    attn_out = jnp.einsum('hqk,kd->hqd', probs_float, value_float)
    delta_rows = lax.optimization_barrier(jnp.sum(cot_float * attn_out, axis=-1))
    value_full = jnp.einsum('hqk,hqd->kd', probs_float, cot_float)
    prob_grad = jnp.einsum('hqd,kd->hqk', cot_float, value_float)
    score_low = (attn_probs * (prob_grad - delta_rows[..., None]) * inv_root).astype(jnp.bfloat16)
    score_float = lax.optimization_barrier(score_low).astype(jnp.float32)
    query_full = jnp.einsum('hqk,kd->hqd', score_float, key_float)
    key_full = jnp.einsum('hqk,hqd->kd', score_float, query_float)
    return (query_full, key_full, value_full)

def one_document(inputs):
    query_doc, key_doc, value_doc, cot_doc = inputs
    group_size = H // KVH
    query_groups = query_doc.reshape(L, KVH, group_size, HD).transpose(1, 2, 0, 3)
    cot_groups = cot_doc.reshape(L, KVH, group_size, HD).transpose(1, 2, 0, 3)
    key_heads = key_doc.reshape(L, KVH, HD).transpose(1, 0, 2)
    value_heads = value_doc.reshape(L, KVH, HD).transpose(1, 0, 2)
    query_full, key_full, value_full = lax.map(head_group, (query_groups, key_heads, value_heads, cot_groups))
    query_rows = query_full.transpose(2, 0, 1, 3).reshape(L, H * HD)
    key_rows = key_full.transpose(1, 0, 2).reshape(L, KVH * HD)
    value_rows = value_full.transpose(1, 0, 2).reshape(L, KVH * HD)
    return (query_rows.astype(jnp.bfloat16), lax.optimization_barrier(jnp.sum(query_rows, axis=0)), key_rows.astype(jnp.bfloat16), lax.optimization_barrier(jnp.sum(key_rows, axis=0)), value_rows.astype(jnp.bfloat16), lax.optimization_barrier(jnp.sum(value_rows, axis=0)))

def reference(query, key_in, value_in, out_grad, masked, bucket):
    positions = jnp.arange(L, dtype=jnp.int32)
    is_masked = jnp.any(masked[:, :, None] == positions[None, None, :], axis=1)
    loss_weight = is_masked.astype(jnp.float32) * NB / (bucket.astype(jnp.float32) + 1.0)
    cotangent = (out_grad.astype(jnp.float32) * loss_weight[:, :, None]).astype(jnp.bfloat16)
    cotangent = lax.optimization_barrier(cotangent)
    results = lax.map(one_document, (query, key_in, value_in, cotangent))
    norm_factor = 1.0 / math.sqrt(DOCS * L)
    bias_query = (lax.optimization_barrier(jnp.sum(results[1], axis=0)) * norm_factor).reshape(N_CTX, H * HD // N_CTX)
    bias_pair = jnp.stack([lax.optimization_barrier(jnp.sum(results[3], axis=0)), lax.optimization_barrier(jnp.sum(results[5], axis=0))]) * norm_factor
    return (results[0], results[2], results[4], bias_query, bias_pair)
```

```python
import functools
import math

import jax
import jax.numpy as jnp
from jax import lax
from jax.experimental import pallas as pl
from jax.experimental.pallas import tpu as pltpu
from jax.sharding import PartitionSpec as P

H = 32
KVH = 8
HD = 128
NB = 16
GROUP = H // KVH
STEP = 2

NT = (((1,), (1,)), ((), ()))
NN = (((1,), (0,)), ((), ()))
TN = (((0,), (0,)), ((), ()))


def dot(a, b, dims):
    return lax.dot_general(a, b, dims, preferred_element_type=jnp.float32)


def attend_kernel(n_pieces, tok, step, doc, n_ctx, *refs):
    place_ref, masked_ref, bucket_ref, query_ref, grad_ref = refs[:5]
    piece_refs = refs[5 : 5 + 2 * n_pieces]
    (dq_ref, near_ref, far_ref, qsum_ref, ksum_ref, vsum_ref, weight_ref) = refs[5 + 2 * n_pieces :]
    inv_root = 1.0 / math.sqrt(HD)

    @pl.when(pl.program_id(0) == 0)
    def _():
        rows = lax.broadcasted_iota(jnp.int32, (tok, masked_ref.shape[1]), 0) + place_ref[0] * tok
        hit = jnp.where(masked_ref[doc : doc + 1, :] == rows, 1.0, 0.0)
        is_masked = jnp.max(hit, axis=1, keepdims=True)
        lane = lax.broadcasted_iota(jnp.int32, (tok, tok), 1)
        line = lax.broadcasted_iota(jnp.int32, (tok, tok), 0)
        spread = jnp.where(lane == line, bucket_ref[doc : doc + 1, :].astype(jnp.float32), 0.0)
        level = jnp.sum(spread, axis=1, keepdims=True)
        weight_ref[...] = jnp.broadcast_to(is_masked * NB / (level + 1.0), weight_ref.shape)

    weight = weight_ref[...]
    for s in range(step):
        cols = [slice((s * GROUP + h) * HD, (s * GROUP + h + 1) * HD) for h in range(GROUP)]
        kv = slice(s * HD, (s + 1) * HD)
        q4 = jnp.concatenate([query_ref[0, :, c] for c in cols], axis=0)
        c4 = jnp.concatenate(
            [(grad_ref[0, :, c].astype(jnp.float32) * weight).astype(jnp.bfloat16) for c in cols],
            axis=0,
        )
        keys = jnp.concatenate([r[:, kv] for r in piece_refs[0::2]], axis=0)
        values = jnp.concatenate([r[:, kv] for r in piece_refs[1::2]], axis=0)
        scores = dot(keys, q4, NT)
        prob_grad = dot(values, c4, NT)
        top = jnp.max(scores, axis=0, keepdims=True)
        expo = jnp.exp((scores - top) * inv_root)
        probs = expo * (1.0 / jnp.sum(expo, axis=0, keepdims=True))
        low = probs.astype(jnp.bfloat16)
        delta = jnp.sum(low.astype(jnp.float32) * prob_grad, axis=0, keepdims=True)
        score_low = (probs * (prob_grad - delta) * inv_root).astype(jnp.bfloat16)
        dv = dot(low, c4, NN)
        dk = dot(score_low, q4, NN)
        dq = dot(score_low, keys, TN)
        for h, c in enumerate(cols):
            part = dq[h * tok : (h + 1) * tok]
            dq_ref[0, :, c] = part.astype(jnp.bfloat16)
            qsum_ref[:, c] = jnp.sum(part, axis=0, keepdims=True)
        ksum_ref[:, kv] = jnp.sum(dk, axis=0, keepdims=True)
        vsum_ref[:, kv] = jnp.sum(dv, axis=0, keepdims=True)
        for which, full in ((0, dk), (1, dv)):
            for piece in range(n_pieces):
                part = full[piece * tok : (piece + 1) * tok]
                if piece % 2:
                    far_ref[piece // 2, which, :, kv] = part.astype(jnp.bfloat16)
                else:
                    near_ref[piece // 2, which, :, kv] = part


def attend(place, masked, bucket, query, out_grad, pieces, doc, n_ctx):
    docs, tok, width = query.shape
    kv_width = KVH * HD
    n_pieces = len(pieces)
    step = STEP
    steps = KVH // step
    qw, kw = step * GROUP * HD, step * HD
    half = n_pieces // 2
    piece_specs, piece_args = [], []
    for piece in pieces:
        piece_specs += [
            pl.BlockSpec((tok, kw), lambda g: (0, g)),
            pl.BlockSpec((tok, kw), lambda g: (0, g + steps)),
        ]
        piece_args += [piece, piece]
    wide = pl.BlockSpec((1, tok, qw), lambda g: (doc, 0, g))
    return pl.pallas_call(
        functools.partial(attend_kernel, n_pieces, tok, step, doc, n_ctx),
        grid=(steps,),
        in_specs=[
            pl.BlockSpec(memory_space=pltpu.SMEM),
            pl.BlockSpec(masked.shape, lambda g: (0, 0)),
            pl.BlockSpec(bucket.shape, lambda g: (0, 0)),
            wide,
            wide,
            *piece_specs,
        ],
        out_specs=[
            pl.BlockSpec((1, tok, qw), lambda g: (0, 0, g)),
            pl.BlockSpec((half, 2, tok, kw), lambda g: (0, 0, 0, g)),
            pl.BlockSpec((half, 2, tok, kw), lambda g: (0, 0, 0, g)),
            pl.BlockSpec((1, qw), lambda g: (0, g)),
            pl.BlockSpec((1, kw), lambda g: (0, g)),
            pl.BlockSpec((1, kw), lambda g: (0, g)),
        ],
        out_shape=[
            jax.ShapeDtypeStruct((1, tok, width), jnp.bfloat16),
            jax.ShapeDtypeStruct((half, 2, tok, kv_width), jnp.float32),
            jax.ShapeDtypeStruct((half, 2, tok, kv_width), jnp.bfloat16),
            jax.ShapeDtypeStruct((1, width), jnp.float32),
            jax.ShapeDtypeStruct((1, kv_width), jnp.float32),
            jax.ShapeDtypeStruct((1, kv_width), jnp.float32),
        ],
        scratch_shapes=[pltpu.VMEM((tok, HD), jnp.float32)],
        name="attend",
    )(place, masked, bucket, query, out_grad, *piece_args)


def per_device(query, key_in, value_in, out_grad, masked, bucket):
    n_ctx = lax.axis_size("ctx")
    n_dp = lax.axis_size("dp")
    docs, tok = query.shape[:2]
    chips = n_ctx // 2
    place = lax.axis_index("ctx").astype(jnp.int32).reshape(1)

    def to_sibling(array):
        return lax.ppermute(array, "ctx", [(i, i ^ 1) for i in range(n_ctx)])

    def shift(array, by):
        return lax.ppermute(array, "ctx", [(i, (i + 2 * by) % n_ctx) for i in range(n_ctx)])

    packed = [jnp.concatenate([key_in[d], value_in[d]], axis=-1) for d in range(docs)]
    away = [[shift(packed[d], s) for s in range(1, chips)] for d in range(docs)]
    query_grads, near, far, qsum, ksum, vsum = [], [], [], 0.0, 0.0, 0.0
    for d in range(docs):
        pieces = [packed[d], to_sibling(packed[d])]
        for other in away[d]:
            pieces += [other, to_sibling(other)]
        dq, here, there, qs, ks, vs = attend(
            place, masked, bucket, query, out_grad, pieces, d, n_ctx
        )
        query_grads.append(dq)
        near.append(here)
        far.append(there)
        qsum, ksum, vsum = (qsum + qs, ksum + ks, vsum + vs)

    grads = []
    for d in range(docs):
        back = to_sibling(far[d])
        total = near[d][0] + back[0].astype(jnp.float32)
        for s in range(1, chips):
            sent = (near[d][s] + back[s].astype(jnp.float32)).astype(jnp.bfloat16)
            total = total + shift(sent, -s).astype(jnp.float32)
        grads.append(total.astype(jnp.bfloat16))
    key_grad = jnp.stack([g[0] for g in grads])
    value_grad = jnp.stack([g[1] for g in grads])

    q_w = H * HD // (n_ctx * n_dp)
    p_w = KVH * HD // n_dp
    q_part = qsum.reshape(n_ctx, n_dp, q_w).transpose(1, 0, 2)
    pair = jnp.stack([ksum.reshape(n_dp, p_w), vsum.reshape(n_dp, p_w)], axis=1)
    pair = jnp.broadcast_to(pair.reshape(n_dp, 1, 2 * p_w), (n_dp, n_ctx, 2 * p_w))
    sends = jnp.concatenate([q_part, pair], axis=-1).reshape(n_dp * n_ctx, q_w + 2 * p_w)
    sums = jnp.sum(lax.all_to_all(sends, ("dp", "ctx"), 0, 0), axis=0)
    norm_factor = 1.0 / math.sqrt(docs * n_dp * tok * n_ctx)
    return (
        jnp.concatenate(query_grads, axis=0),
        key_grad,
        value_grad,
        (sums[:q_w] * norm_factor).reshape(1, q_w),
        (sums[q_w:] * norm_factor).reshape(2, p_w),
    )


def solution(mesh):
    in_specs = (
        P("dp", "ctx", None),
        P("dp", "ctx", None),
        P("dp", "ctx", None),
        P("dp", "ctx", None),
        P("dp", None),
        P("dp", "ctx"),
    )
    out_specs = (
        P("dp", "ctx", None),
        P("dp", "ctx", None),
        P("dp", "ctx", None),
        P("ctx", "dp"),
        P(None, "dp"),
    )
    return jax.shard_map(
        per_device, mesh=mesh, in_specs=in_specs, out_specs=out_specs, check_vma=False
    )
```

```python
import functools
import math

import jax
import jax.numpy as jnp
from jax import lax
from jax.experimental import pallas as pl
from jax.experimental.pallas import tpu as pltpu
from jax.sharding import PartitionSpec as P


H = 32
KVH = 8
HD = 128
NB = 16
GROUP = H // KVH
CORES = 2
HEADS = KVH // CORES
QW = HEADS * GROUP * HD
KW = HEADS * HD

NT = (((1,), (1,)), ((), ()))
NN = (((1,), (0,)), ((), ()))
TN = (((0,), (0,)), ((), ()))
BF = jnp.bfloat16
F32 = jnp.float32


def dot(a, b, dims):
    return lax.dot_general(a, b, dims, preferred_element_type=F32)


def whole(shape):
    return pl.BlockSpec(shape, lambda *_: (0,) * len(shape))


HELD_CTX = 4


def fits(n_ctx):
    return n_ctx <= HELD_CTX


def vmem(shape, dtype):
    if fits(lax.axis_size("ctx")):
        return pltpu.VMEM(shape, dtype)
    return jax.ShapeDtypeStruct(shape, dtype)


def held(array):
    if fits(lax.axis_size("ctx")):
        return pltpu.with_memory_space_constraint(array, pltpu.VMEM)
    return array


def grant(mib):
    if fits(lax.axis_size("ctx")):
        return pltpu.CompilerParams(vmem_limit_bytes=mib << 20)
    return None


IN_VMEM = pl.BlockSpec(memory_space=pltpu.VMEM)
IN_SMEM = pl.BlockSpec(memory_space=pltpu.SMEM)


def split_kv_kernel(place_ref, key_mine, value_mine, key_other, value_other, *outs):
    docs = key_mine.shape[0]
    for d in range(docs):
        outs[2 * d][0] = key_mine[d]
        outs[2 * d][1] = value_mine[d]
        outs[2 * d + 1][0] = key_other[d]
        outs[2 * d + 1][1] = value_other[d]


def split_kv(place, key_in, value_in):
    docs, tok = key_in.shape[:2]
    mine = pl.BlockSpec((docs, tok, KW), lambda g, p: (0, 0, p[0] % CORES))
    other = pl.BlockSpec((docs, tok, KW), lambda g, p: (0, 0, 1 - p[0] % CORES))
    shape = (2, tok, KW)
    outs = pl.pallas_call(
        split_kv_kernel,
        grid_spec=pltpu.PrefetchScalarGridSpec(
            num_scalar_prefetch=1,
            grid=(1,),
            in_specs=[mine, mine, other, other],
            out_specs=[IN_VMEM] * (2 * docs),
        ),
        out_shape=[vmem(shape, BF)] * (2 * docs),
        compiler_params=grant(4),
        name="split_kv",
    )(place, key_in, value_in, key_in, value_in)
    return outs[0::2], outs[1::2]


def weigh_kernel(
    place_ref, masked_ref, bucket_ref, query_own, grad_own, query_ref, grad_ref, *outs
):
    docs, tok = query_ref.shape[:2]
    rows = lax.broadcasted_iota(jnp.int32, (tok, masked_ref.shape[1]), 0) + place_ref[0] * tok
    lane = lax.broadcasted_iota(jnp.int32, (tok, tok), 1)
    line = lax.broadcasted_iota(jnp.int32, (tok, tok), 0)
    for d in range(docs):
        hit = jnp.where(masked_ref[d : d + 1, :] == rows, 1.0, 0.0)
        is_masked = jnp.max(hit, axis=1, keepdims=True)
        spread = jnp.where(lane == line, bucket_ref[d : d + 1, :].astype(F32), 0.0)
        level = jnp.sum(spread, axis=1, keepdims=True)
        weight = is_masked * NB / (level + 1.0)
        outs[2 * d][0] = query_own[d]
        outs[2 * d][1] = (grad_own[d].astype(F32) * weight).astype(BF)
        outs[2 * d + 1][0] = query_ref[d]
        outs[2 * d + 1][1] = (grad_ref[d].astype(F32) * weight).astype(BF)


def weigh(place, masked, bucket, query, out_grad):
    docs, tok = query.shape[:2]
    own = pl.BlockSpec((docs, tok, QW), lambda g, p: (0, 0, p[0] % CORES))
    other = pl.BlockSpec((docs, tok, QW), lambda g, p: (0, 0, 1 - p[0] % CORES))
    outs = pl.pallas_call(
        weigh_kernel,
        grid_spec=pltpu.PrefetchScalarGridSpec(
            num_scalar_prefetch=1,
            grid=(1,),
            in_specs=[whole(masked.shape), whole(bucket.shape), own, own, other, other],
            out_specs=[IN_VMEM] * (2 * docs),
        ),
        out_shape=[vmem((2, tok, QW), BF)] * (2 * docs),
        compiler_params=grant(8),
        name="weigh",
    )(place, masked, bucket, query, out_grad, query, out_grad)
    return outs[0::2], outs[1::2]


def attend_kernel(n_pieces, tok, has_before, own_ref, swap_ref, *refs):
    piece_refs = refs[:n_pieces]
    before_refs = refs[n_pieces : n_pieces + 2 * has_before]
    dq_ref, dq_sib_ref, qsum_ref, kvsum_ref, near_ref, *far_refs = refs[
        n_pieces + 2 * has_before :
    ]
    inv_root = 1.0 / math.sqrt(HD)
    for g in range(HEADS):
        cols = [slice((g * GROUP + h) * HD, (g * GROUP + h + 1) * HD) for h in range(GROUP)]
        kv = slice(g * HD, (g + 1) * HD)
        q_rows, c_rows = (
            jnp.concatenate([ref[which, :, c] for ref in (own_ref, swap_ref) for c in cols], axis=0)
            for which in (0, 1)
        )
        keys, values = (
            jnp.concatenate([r[which, :, kv] for r in piece_refs], axis=0) for which in (0, 1)
        )
        scores = dot(keys, q_rows, NT)
        prob_grad = dot(values, c_rows, NT)
        top = jnp.max(scores, axis=0, keepdims=True)
        expo = jnp.exp((scores - top) * inv_root)
        probs = expo * (1.0 / jnp.sum(expo, axis=0, keepdims=True))
        low = probs.astype(BF)
        delta = jnp.sum(low.astype(F32) * prob_grad, axis=0, keepdims=True)
        score_low = (probs * (prob_grad - delta) * inv_root).astype(BF)
        dv = dot(low, c_rows, NN)
        dk = dot(score_low, q_rows, NN)
        dq = dot(score_low, keys, TN)
        for h, c in enumerate(cols):
            part = dq[h * tok : (h + 1) * tok]
            other = dq[(GROUP + h) * tok : (GROUP + h + 1) * tok]
            dq_ref[:, c] = part.astype(BF)
            dq_sib_ref[:, c] = other.astype(BF)
            row = g * GROUP + h
            total = jnp.sum(part + other, axis=0, keepdims=True)
            if has_before:
                total = total + before_refs[0][row : row + 1]
            qsum_ref[row : row + 1] = total
        for which, full in ((0, dk), (1, dv)):
            side = slice(which * HD, (which + 1) * HD)
            total = jnp.sum(full, axis=0, keepdims=True)
            if has_before:
                total = total + before_refs[1][g : g + 1, side]
            kvsum_ref[g : g + 1, side] = total
            near_ref[which, :, kv] = full[:tok]
            for piece in range(1, n_pieces):
                part = full[piece * tok : (piece + 1) * tok]
                far_refs[piece - 1][which, :, kv] = part.astype(BF)


def attend(own, swap, pieces, before):
    tok = own.shape[1]
    n_pieces = len(pieces)
    args = [own, swap, *pieces, *before]
    outs = pl.pallas_call(
        functools.partial(attend_kernel, n_pieces, tok, bool(before)),
        in_specs=[IN_VMEM] * len(args),
        out_specs=[IN_VMEM] * (5 + n_pieces - 1),
        out_shape=[
            vmem((tok, QW), BF),
            vmem((tok, QW), BF),
            vmem((HEADS * GROUP, HD), F32),
            vmem((HEADS, 2 * HD), F32),
            vmem((2, tok, KW), F32),
            *[vmem((2, tok, KW), BF)] * (n_pieces - 1),
        ],
        compiler_params=grant(20),
        name="attend",
    )(*[held(arg) for arg in args])
    return outs[:2], outs[2:4], outs[4], outs[5:]


def share_kernel(n_ctx, n_dp, place_ref, qsum_ref, kvsum_ref, out_ref):
    for core in range(CORES):

        @pl.when(place_ref[0] % CORES == core)
        def _():
            out_ref[...] = jnp.zeros(out_ref.shape, F32)
            base = core * H // CORES
            for row in range(HEADS * GROUP):
                out_ref[base + row, :, :HD] = qsum_ref[row : row + 1]
            for c in range(n_ctx):
                for g in range(HEADS):
                    out_ref[c * n_dp + core * HEADS + g, :, HD:] = kvsum_ref[g : g + 1]


def shares_of(place, sums, n_ctx, n_dp):
    qsum, kvsum = sums
    q_w = H * HD // (n_ctx * n_dp)
    p_w = KVH * HD // n_dp
    rows = n_ctx * n_dp
    if q_w == HD and p_w == HD:
        return pl.pallas_call(
            functools.partial(share_kernel, n_ctx, n_dp),
            in_specs=[IN_SMEM, IN_VMEM, IN_VMEM],
            out_specs=IN_VMEM,
            out_shape=vmem((rows, 1, q_w + 2 * p_w), F32),
            compiler_params=grant(2),
            name="share",
        )(place, held(qsum), held(kvsum))
    core = place[0] % CORES

    def both_halves(part):
        return jnp.concatenate([jnp.where(core == c, part, 0.0) for c in range(CORES)], axis=0)

    q_part = both_halves(qsum).reshape(n_ctx, n_dp, q_w)
    pair = both_halves(kvsum)
    pair = jnp.concatenate(
        [pair[:, :HD].reshape(n_dp, p_w), pair[:, HD:].reshape(n_dp, p_w)], axis=1
    )
    pair = jnp.broadcast_to(pair[None], (n_ctx, n_dp, 2 * p_w))
    return jnp.concatenate([q_part, pair], axis=-1).reshape(rows, 1, q_w + 2 * p_w)


def join_q_kernel(docs, place_ref, *refs):
    out_ref = refs[2 * docs]
    for core in range(CORES):

        @pl.when(place_ref[0] % CORES == core)
        def _():
            mine, other = (slice(c * QW, (c + 1) * QW) for c in (core, 1 - core))
            for d in range(docs):
                out_ref[d, :, mine] = refs[2 * d][...]
                out_ref[d, :, other] = refs[2 * d + 1][...]


def join_q(place, parts):
    docs, tok = len(parts), parts[0][0].shape[0]
    shape = (docs, tok, CORES * QW)
    return pl.pallas_call(
        functools.partial(join_q_kernel, docs),
        in_specs=[IN_SMEM] + [IN_VMEM] * (2 * docs),
        out_shape=jax.ShapeDtypeStruct(shape, BF),
        compiler_params=grant(6),
        name="join_q",
    )(place, *[held(part) for pair in parts for part in pair])


def join_kv_kernel(docs, terms, place_ref, *refs):
    key_ref, value_ref = refs[2 * docs * terms :]
    for core in range(CORES):

        @pl.when(place_ref[0] % CORES == core)
        def _():
            for d in range(docs):
                for side, half in ((0, core), (1, 1 - core)):
                    first = (2 * d + side) * terms
                    total = refs[first][...].astype(F32)
                    for ref in refs[first + 1 : first + terms]:
                        total = total + ref[...].astype(F32)
                    cols = slice(half * KW, (half + 1) * KW)
                    key_ref[d, :, cols] = total[0].astype(BF)
                    value_ref[d, :, cols] = total[1].astype(BF)


def join_kv(place, parts):
    docs, terms, tok = len(parts), len(parts[0][0]), parts[0][0][0].shape[1]
    shape = jax.ShapeDtypeStruct((docs, tok, CORES * KW), BF)
    flat = [held(part) for sides in parts for side in sides for part in side]
    return pl.pallas_call(
        functools.partial(join_kv_kernel, docs, terms),
        in_specs=[IN_SMEM] + [IN_VMEM] * len(flat),
        out_shape=[shape, shape],
        compiler_params=grant(6),
        name="join_kv",
    )(place, *flat)


def bias_kernel(norm_factor, q_w, p_w, gathered_ref, query_ref, pair_ref):
    totals = jnp.sum(gathered_ref[...], axis=0) * norm_factor
    query_ref[...] = totals[:, :q_w]
    pair_ref[0:1] = totals[:, q_w : q_w + p_w]
    pair_ref[1:2] = totals[:, q_w + p_w :]


def bias_out(gathered, norm_factor, q_w, p_w):
    return pl.pallas_call(
        functools.partial(bias_kernel, norm_factor, q_w, p_w),
        in_specs=[IN_VMEM],
        out_shape=[
            jax.ShapeDtypeStruct((1, q_w), F32),
            jax.ShapeDtypeStruct((2, p_w), F32),
        ],
        compiler_params=grant(2),
        name="bias_out",
    )(held(gathered))


def hops_of(n_ctx):
    return [(s, x) for s in range(n_ctx // CORES) for x in range(CORES) if s or x]


def step_device(query, key_in, value_in, out_grad, masked, bucket):
    n_ctx = lax.axis_size("ctx")
    n_dp = lax.axis_size("dp")
    docs, tok = query.shape[:2]
    chips = n_ctx // CORES
    hops = hops_of(n_ctx)
    place = lax.axis_index("ctx").astype(jnp.int32).reshape(1)

    def move(array, chip, cross):
        pairs = [(i, (i + CORES * chip) % n_ctx ^ cross) for i in range(n_ctx)]
        return lax.ppermute(array, "ctx", pairs)

    mine, other = split_kv(place, key_in, value_in)
    pieces = [
        [mine[d]] + [move((mine, other)[x][d], s, x) for s, x in hops]
        for d in range(docs)
    ]
    own, sends = weigh(place, masked, bucket, query, out_grad)
    swaps = [move(send, 0, 1) for send in sends]
    q_parts, kv_parts, sums = [], [], ()
    for d in range(docs):
        (dq, dq_sib), sums, near, far = attend(own[d], swaps[d], pieces[d], sums)
        back = {(s, x): move(part, -s, x) for (s, x), part in zip(hops, far)}
        kv_parts.append(
            [
                [near] + [back[s, 0] for s in range(1, chips)],
                [back[s, 1] for s in range(chips)],
            ]
        )
        q_parts.append((dq, move(dq_sib, 0, 1)))

    shares = shares_of(place, sums, n_ctx, n_dp)
    gathered = lax.all_to_all(shares, ("ctx", "dp"), 0, 0)
    norm_factor = 1.0 / math.sqrt(docs * n_dp * tok * n_ctx)
    q_w = H * HD // (n_ctx * n_dp)
    p_w = KVH * HD // n_dp
    key_grad, value_grad = join_kv(place, kv_parts)
    query_grad = join_q(place, q_parts)
    bias_q, bias_kv = bias_out(gathered, norm_factor, q_w, p_w)
    return query_grad, key_grad, value_grad, bias_q, bias_kv


def solution(mesh):
    in_specs = (
        P("dp", "ctx", None),
        P("dp", "ctx", None),
        P("dp", "ctx", None),
        P("dp", "ctx", None),
        P("dp", None),
        P("dp", "ctx"),
    )
    out_specs = (
        P("dp", "ctx", None),
        P("dp", "ctx", None),
        P("dp", "ctx", None),
        P("ctx", "dp"),
        P(None, "dp"),
    )
    return jax.shard_map(
        step_device, mesh=mesh, in_specs=in_specs, out_specs=out_specs, check_vma=False
    )
```

```python
import functools
import math

import jax
import jax.numpy as jnp
from jax import lax
from jax.experimental import pallas as pl
from jax.experimental.pallas import tpu as pltpu
from jax.sharding import PartitionSpec as P


H = 32
KVH = 8
HD = 128
NB = 16
GROUP = H // KVH
CORES = 2
HEADS = KVH // CORES
QW = HEADS * GROUP * HD
KW = HEADS * HD

NT = (((1,), (1,)), ((), ()))
NN = (((1,), (0,)), ((), ()))
TN = (((0,), (0,)), ((), ()))
BF = jnp.bfloat16
F32 = jnp.float32


def dot(a, b, dims):
    return lax.dot_general(a, b, dims, preferred_element_type=F32)


def whole(shape):
    return pl.BlockSpec(shape, lambda *_: (0,) * len(shape))


HELD_CTX = 4


def fits(n_ctx):
    return n_ctx <= HELD_CTX


def vmem(shape, dtype):
    if fits(lax.axis_size("ctx")):
        return pltpu.VMEM(shape, dtype)
    return jax.ShapeDtypeStruct(shape, dtype)


def held(array):
    if fits(lax.axis_size("ctx")):
        return pltpu.with_memory_space_constraint(array, pltpu.VMEM)
    return array


def in_hbm(array):
    if fits(lax.axis_size("ctx")):
        return pltpu.with_memory_space_constraint(array, pltpu.HBM)
    return array


def grant(mib):
    if fits(lax.axis_size("ctx")):
        return pltpu.CompilerParams(vmem_limit_bytes=mib << 20)
    return None


IN_VMEM = pl.BlockSpec(memory_space=pltpu.VMEM)
IN_SMEM = pl.BlockSpec(memory_space=pltpu.SMEM)


def chunks_of(docs):
    mid = HEADS // 2
    return [(d, 0, HEADS) for d in range(docs - 1)] + [(docs - 1, 0, mid), (docs - 1, mid, HEADS)]


def returns_of(docs):
    last = len(chunks_of(docs)) - 1
    return [[n] for n in range(last - 2)] + [[last - 2, last - 1], [last]]


def split_kv_kernel(chunks, place_ref, key_ref, value_ref, *refs):
    outs, sems = refs[:-1], refs[-1]
    core = place_ref[0] % CORES
    copies = []
    for n, (d, lo, hi) in enumerate(chunks):
        for side, half in ((0, core), (1, 1 - core)):
            start = pl.multiple_of(half * KW + lo * HD, HD)
            for which, ref in ((0, key_ref), (1, value_ref)):
                copies.append(
                    pltpu.make_async_copy(
                        ref.at[d, :, pl.ds(start, (hi - lo) * HD)],
                        outs[2 * n + side].at[which],
                        sems.at[len(copies)],
                    )
                )
    for copy in copies:
        copy.start()
    for copy in copies:
        copy.wait()


def split_kv(place, key_in, value_in):
    docs, tok = key_in.shape[:2]
    chunks = chunks_of(docs)
    shapes = [(2, tok, (hi - lo) * HD) for _, lo, hi in chunks for _ in range(2)]
    outs = pl.pallas_call(
        functools.partial(split_kv_kernel, chunks),
        in_specs=[IN_SMEM, pl.BlockSpec(memory_space=pl.ANY), pl.BlockSpec(memory_space=pl.ANY)],
        out_specs=[IN_VMEM] * len(shapes),
        out_shape=[vmem(shape, BF) for shape in shapes],
        scratch_shapes=[pltpu.SemaphoreType.DMA((2 * len(shapes),))],
        compiler_params=grant(4),
        name="split_kv",
    )(place, in_hbm(key_in), in_hbm(value_in))
    return outs[0::2], outs[1::2]


def weigh_kernel(
    place_ref, masked_ref, bucket_ref, query_own, grad_own, query_ref, grad_ref, *outs
):
    docs, tok = query_ref.shape[:2]
    rows = lax.broadcasted_iota(jnp.int32, (tok, masked_ref.shape[1]), 0) + place_ref[0] * tok
    lane = lax.broadcasted_iota(jnp.int32, (tok, tok), 1)
    line = lax.broadcasted_iota(jnp.int32, (tok, tok), 0)
    for d in range(docs):
        hit = jnp.where(masked_ref[d : d + 1, :] == rows, 1.0, 0.0)
        is_masked = jnp.max(hit, axis=1, keepdims=True)
        spread = jnp.where(lane == line, bucket_ref[d : d + 1, :].astype(F32), 0.0)
        level = jnp.sum(spread, axis=1, keepdims=True)
        weight = is_masked * NB / (level + 1.0)
        outs[2 * d][0] = query_own[d]
        outs[2 * d][1] = (grad_own[d].astype(F32) * weight).astype(BF)
        outs[2 * d + 1][0] = query_ref[d]
        outs[2 * d + 1][1] = (grad_ref[d].astype(F32) * weight).astype(BF)


def weigh(place, masked, bucket, query, out_grad):
    docs, tok = query.shape[:2]
    own = pl.BlockSpec((docs, tok, QW), lambda g, p: (0, 0, p[0] % CORES))
    other = pl.BlockSpec((docs, tok, QW), lambda g, p: (0, 0, 1 - p[0] % CORES))
    outs = pl.pallas_call(
        weigh_kernel,
        grid_spec=pltpu.PrefetchScalarGridSpec(
            num_scalar_prefetch=1,
            grid=(1,),
            in_specs=[whole(masked.shape), whole(bucket.shape), own, own, other, other],
            out_specs=[IN_VMEM] * (2 * docs),
        ),
        out_shape=[vmem((2, tok, QW), BF)] * (2 * docs),
        compiler_params=grant(8),
        name="weigh",
    )(place, masked, bucket, *[in_hbm(a) for a in (query, out_grad, query, out_grad)])
    return outs[0::2], outs[1::2]


def attend_kernel(n_pieces, tok, lo, hi, skip, before, n_dp, place_ref, own_ref, swap_ref, *refs):
    piece_refs, refs = refs[:n_pieces], refs[n_pieces:]
    if skip:
        carry_refs, refs = refs[:n_pieces], refs[n_pieces:]
    before_refs, refs = refs[: 2 * len(before)], refs[2 * len(before) :]
    dq_ref, dq_sib_ref, *refs = refs
    qsum_ref, kvsum_ref, near_ref, *far_refs = refs
    inv_root = 1.0 / math.sqrt(HD)
    if skip:
        dq_sib_ref[:, : skip * GROUP * HD] = carry_refs[0][...]
        for far_ref, carry_ref in zip(far_refs, carry_refs[1:]):
            far_ref[:, :, : skip * HD] = carry_ref[...]
    for g in range(lo, hi):
        cols = [slice((g * GROUP + h) * HD, (g * GROUP + h + 1) * HD) for h in range(GROUP)]
        kv = slice((g - lo) * HD, (g - lo + 1) * HD)
        kv_out = slice((g - lo + skip) * HD, (g - lo + skip + 1) * HD)
        q_rows, c_rows = (
            jnp.concatenate([ref[which, :, c] for ref in (own_ref, swap_ref) for c in cols], axis=0)
            for which in (0, 1)
        )
        keys, values = (
            jnp.concatenate([r[which, :, kv] for r in piece_refs], axis=0) for which in (0, 1)
        )
        scores = dot(keys, q_rows, NT)
        prob_grad = dot(values, c_rows, NT)
        top = jnp.max(scores, axis=0, keepdims=True)
        expo = jnp.exp((scores - top) * inv_root)
        probs = expo * (1.0 / jnp.sum(expo, axis=0, keepdims=True))
        low = probs.astype(BF)
        delta = jnp.sum(low.astype(F32) * prob_grad, axis=0, keepdims=True)
        score_low = (probs * (prob_grad - delta) * inv_root).astype(BF)
        dv = dot(low, c_rows, NN)
        dk = dot(score_low, q_rows, NN)
        dq = dot(score_low, keys, TN)
        for h in range(GROUP):
            row = (g - lo) * GROUP + h
            c = slice(row * HD, (row + 1) * HD)
            part = dq[h * tok : (h + 1) * tok]
            other = dq[(GROUP + h) * tok : (GROUP + h + 1) * tok]
            dq_ref[:, c] = part.astype(BF)
            out = row + skip * GROUP
            dq_sib_ref[:, out * HD : (out + 1) * HD] = other.astype(BF)
            qsum_ref[row : row + 1] = jnp.sum(part + other, axis=0, keepdims=True)
        for which, full in ((0, dk), (1, dv)):
            side = slice(which * HD, (which + 1) * HD)
            kvsum_ref[g - lo : g - lo + 1, side] = jnp.sum(full, axis=0, keepdims=True)
            near_ref[which, :, kv] = full[:tok]
            for piece in range(1, n_pieces):
                part = full[piece * tok : (piece + 1) * tok]
                far_refs[piece - 1][which, :, kv_out] = part.astype(BF)
    if before:
        share_ref = far_refs[n_pieces - 1]
        sums = [(lo, hi, qsum_ref, kvsum_ref)]
        sums += [(a, b, *before_refs[2 * i : 2 * i + 2]) for i, (a, b) in enumerate(before)]
        core = place_ref[0] % CORES
        share_ref[...] = jnp.zeros(share_ref.shape, F32)
        for g in range(HEADS):
            here = [(g - a, q, kv) for a, b, q, kv in sums if a <= g < b]
            for h in range(GROUP):
                rows = [q[i * GROUP + h : i * GROUP + h + 1] for i, q, _ in here]
                share_ref[core * (HEADS * GROUP) + g * GROUP + h, :, :HD] = sum(rows[1:], rows[0])
            rows = [kv[i : i + 1] for i, _, kv in here]
            total = sum(rows[1:], rows[0])
            for c in range(share_ref.shape[0] // n_dp):
                share_ref[c * n_dp + core * HEADS + g, :, HD:] = total


def attend(place, own, swap, pieces, lo, hi, carry, before, ranges, n_dp, rows):
    tok = own.shape[1]
    n_pieces = len(pieces)
    heads = hi - lo
    skip = carry[1].shape[2] // HD if carry else 0
    args = [own, swap, *pieces, *carry, *[part for pair in before for part in pair]]
    out_shape = [
        vmem((tok, heads * GROUP * HD), BF),
        vmem((tok, (heads + skip) * GROUP * HD), BF),
        vmem((heads * GROUP, HD), F32),
        vmem((heads, 2 * HD), F32),
        vmem((2, tok, heads * HD), F32),
        *[vmem((2, tok, (heads + skip) * HD), BF)] * (n_pieces - 1),
    ]
    if before:
        out_shape.append(jax.ShapeDtypeStruct((rows, 1, 3 * HD), F32))
    ranges = ranges if before else []
    outs = pl.pallas_call(
        functools.partial(attend_kernel, n_pieces, tok, lo, hi, skip, ranges, n_dp),
        in_specs=[IN_SMEM] + [IN_VMEM] * len(args),
        out_specs=[IN_VMEM] * len(out_shape),
        out_shape=out_shape,
        compiler_params=grant(20),
        name="attend",
    )(place, *[held(arg) for arg in args])
    return outs[:2], outs[2:4], outs[4], outs[5 : 4 + n_pieces], outs[-1]


def shares_of(place, sums, chunks, n_ctx, n_dp):
    q_w = H * HD // (n_ctx * n_dp)
    p_w = KVH * HD // n_dp
    core = place[0] % CORES
    qsum = jnp.zeros((HEADS * GROUP, HD), F32)
    kvsum = jnp.zeros((HEADS, 2 * HD), F32)
    for (_, lo, hi), (q, kv) in zip(chunks, sums):
        qsum = qsum.at[lo * GROUP : hi * GROUP].add(q)
        kvsum = kvsum.at[lo:hi].add(kv)

    def both_halves(part):
        return jnp.concatenate([jnp.where(core == c, part, 0.0) for c in range(CORES)], axis=0)

    q_part = both_halves(qsum).reshape(n_ctx, n_dp, q_w)
    pair = both_halves(kvsum)
    pair = jnp.concatenate(
        [pair[:, :HD].reshape(n_dp, p_w), pair[:, HD:].reshape(n_dp, p_w)], axis=1
    )
    pair = jnp.broadcast_to(pair[None], (n_ctx, n_dp, 2 * p_w))
    return jnp.concatenate([q_part, pair], axis=-1).reshape(n_ctx * n_dp, 1, q_w + 2 * p_w)


def place_of(n, docs):
    chunks = chunks_of(docs)
    for i, group in enumerate(returns_of(docs)):
        if n in group:
            ahead = group[: group.index(n)]
            return i, sum(chunks[m][2] - chunks[m][1] for m in ahead)


def join_q_kernel(docs, place_ref, *refs):
    chunks = chunks_of(docs)
    out_ref, near_refs, far_refs = refs[-1], refs[: len(chunks)], refs[len(chunks) : -1]
    width = GROUP * HD
    for core in range(CORES):

        @pl.when(place_ref[0] % CORES == core)
        def _():
            for n, (d, lo, hi) in enumerate(chunks):
                mine, other = (half * HEADS + lo for half in (core, 1 - core))
                i, ahead = place_of(n, docs)
                heads = hi - lo
                out_ref[d, :, mine * width : (mine + heads) * width] = near_refs[n][...]
                out_ref[d, :, other * width : (other + heads) * width] = far_refs[i][
                    :, ahead * width : (ahead + heads) * width
                ]


def join_q(place, near, far, docs):
    tok = near[0].shape[0]
    args = near + far
    return pl.pallas_call(
        functools.partial(join_q_kernel, docs),
        in_specs=[IN_SMEM] + [IN_VMEM] * len(args),
        out_shape=jax.ShapeDtypeStruct((docs, tok, CORES * QW), BF),
        compiler_params=grant(6),
        name="join_q",
    )(place, *[held(arg) for arg in args])


def join_kv_kernel(docs, chips, place_ref, *refs):
    chunks = chunks_of(docs)
    *refs, key_ref, value_ref = refs
    near_refs, back_refs = refs[: len(chunks)], refs[len(chunks) :]
    per_group = CORES * chips - 1
    for core in range(CORES):

        @pl.when(place_ref[0] % CORES == core)
        def _():
            for n, (d, lo, hi) in enumerate(chunks):
                i, ahead = place_of(n, docs)
                cols = slice(ahead * HD, (ahead + hi - lo) * HD)
                back = back_refs[i * per_group : (i + 1) * per_group]
                hops = hops_of(CORES * chips)
                for side, half in ((0, core), (1, 1 - core)):
                    terms = [ref[:, :, cols].astype(F32) for ref, (_, x) in zip(back, hops) if x == side]
                    if side == 0:
                        terms.append(near_refs[n][...])
                    total = sum(terms[1:], terms[0])
                    out = slice((half * HEADS + lo) * HD, (half * HEADS + hi) * HD)
                    key_ref[d, :, out] = total[0].astype(BF)
                    value_ref[d, :, out] = total[1].astype(BF)


def join_kv(place, near, back, docs, chips):
    tok = near[0].shape[1]
    shape = jax.ShapeDtypeStruct((docs, tok, CORES * KW), BF)
    args = near + [part for group in back for part in group]
    return pl.pallas_call(
        functools.partial(join_kv_kernel, docs, chips),
        in_specs=[IN_SMEM] + [IN_VMEM] * len(args),
        out_shape=[shape, shape],
        compiler_params=grant(6),
        name="join_kv",
    )(place, *[held(arg) for arg in args])


def bias_kernel(norm_factor, gathered_ref, query_ref, pair_ref):
    q_w, p_w = query_ref.shape[1], pair_ref.shape[1]
    totals = jnp.sum(gathered_ref[...], axis=0) * norm_factor
    query_ref[...] = totals[:, :q_w]
    pair_ref[0:1] = totals[:, q_w : q_w + p_w]
    pair_ref[1:2] = totals[:, q_w + p_w :]


def bias_out(gathered, norm_factor, q_w, p_w):
    return pl.pallas_call(
        functools.partial(bias_kernel, norm_factor),
        in_specs=[IN_VMEM],
        out_shape=[
            jax.ShapeDtypeStruct((1, q_w), F32),
            jax.ShapeDtypeStruct((2, p_w), F32),
        ],
        compiler_params=grant(2),
        name="bias_out",
    )(held(gathered))


def hops_of(n_ctx):
    return [(s, x) for s in range(1, n_ctx // CORES) for x in range(CORES)] + [(0, 1)]


def step_device(query, key_in, value_in, out_grad, masked, bucket):
    n_ctx = lax.axis_size("ctx")
    n_dp = lax.axis_size("dp")
    docs, tok = query.shape[:2]
    chips = n_ctx // CORES
    hops = hops_of(n_ctx)
    chunks = chunks_of(docs)
    q_w = H * HD // (n_ctx * n_dp)
    p_w = KVH * HD // n_dp
    in_rows = q_w == HD and p_w == HD
    place = lax.axis_index("ctx").astype(jnp.int32).reshape(1)

    def move(array, chip, cross):
        pairs = [(i, (i + CORES * chip) % n_ctx ^ cross) for i in range(n_ctx)]
        return lax.ppermute(array, "ctx", pairs)

    mine, other = split_kv(place, key_in, value_in)
    pieces = [
        [mine[n]] + [move((mine, other)[x][n], s, x) for s, x in hops]
        for n in range(len(chunks))
    ]
    own, sends = weigh(place, masked, bucket, query, out_grad)
    swaps = [move(send, 0, 1) for send in sends]
    groups = returns_of(docs)
    near_q, far_q, near_kv, back_kv, sums, carry = [], [], [], [], [], []
    for n, (d, lo, hi) in enumerate(chunks):
        before = sums if in_rows and n == len(chunks) - 1 else []
        ranges = [chunk[1:] for chunk in chunks[:n]]
        (dq, dq_sib), sums_n, near, far, share = attend(
            place, own[d], swaps[d], pieces[n], lo, hi, carry, before, ranges, n_dp, n_ctx * n_dp
        )
        near_q.append(dq)
        near_kv.append(near)
        sums = sums + [sums_n]
        i = place_of(n, docs)[0]
        if n < groups[i][-1]:
            carry = [dq_sib, *far]
            continue
        carry = []
        back_kv.append([move(part, -s, x) for (s, x), part in zip(hops, far)])
        far_q.append(move(dq_sib, 0, 1))

    if not in_rows:
        share = shares_of(place, sums, chunks, n_ctx, n_dp)
    gathered = lax.all_to_all(share, ("ctx", "dp"), 0, 0)
    norm_factor = 1.0 / math.sqrt(docs * n_dp * tok * n_ctx)
    key_grad, value_grad = join_kv(place, near_kv, back_kv, docs, chips)
    query_grad = join_q(place, near_q, far_q, docs)
    bias_q, bias_kv = bias_out(gathered, norm_factor, q_w, p_w)
    return query_grad, key_grad, value_grad, bias_q, bias_kv


def solution(mesh):
    in_specs = (
        P("dp", "ctx", None),
        P("dp", "ctx", None),
        P("dp", "ctx", None),
        P("dp", "ctx", None),
        P("dp", None),
        P("dp", "ctx"),
    )
    out_specs = (
        P("dp", "ctx", None),
        P("dp", "ctx", None),
        P("dp", "ctx", None),
        P("ctx", "dp"),
        P(None, "dp"),
    )
    return jax.shard_map(
        step_device, mesh=mesh, in_specs=in_specs, out_specs=out_specs, check_vma=False
    )
```
